32 devices in a mesh: groups: 2 (over y), ctx: 4 (over z), head: 2 (over x), rep: 2 (over core).
Axes of the slice: x: 2, y: 2, z: 4, core: 2. Of those that a mesh axis runs over, the one named last changes fastest.
Arguments:
- queries: bfloat16 [8192, 16, 2, 128], P(('groups', 'ctx'), 'head', 'rep'), parts along dimension 0, may hold values from -10 to 10
- keys_values: bfloat16 [2, 8192, 16, 128], P('rep', ('groups', 'ctx'), 'head'), parts along dimension 1, may hold values from -6 to 6
- far_list: int32 [64, 16], P('groups'), parts along dimension 0, may hold values from 0 to 31, as said below
- far_count: int32 [64], P('groups'), parts along dimension 0, may hold values from 0 to 8
Outputs:
- attended: bfloat16 [8192, 16, 2, 128], P(('groups', 'ctx'), 'head', 'rep'), parts along dimension 0
The draws below stay inside these ranges and needn't reach their ends.
There are 2 independent parts, one for each index of `groups`. The reference program is written for one: setup_inputs(seed, part) draws one part's arguments, and reference() takes and returns one part's arrays. A program takes and returns all parts, laid end to end along the dimension named above; each array names one. Nothing has to cross between parts.
Inputs may be any that keep to these rules, and one draw needn't show every extreme that they name: `far_list`: for query block c, the entries j < far_count[c] are distinct block numbers no later than c - 4; entries from far_count[c] on are arbitrary and not read. Taken over all query blocks of one span of 1024 tokens, the counted entries name at most 2 distinct blocks of any one span, and some span's query blocks name exactly 2 of some span in every draw.
All inputs are finite; a program needn't handle non-finite values.
Results may differ from the reference program's by a relative error of at most 0.003.
Values may be sent and summed in bfloat16 or wider, within the bound.
A program may use at most 128 MiB of HBM per device.

```python
import jax
import jax.numpy as jnp
from jax import lax

DH = 128
KVH = 16
GQA = 2
BLK = 128
WB = 4
FSEL = 16
CAP = 2
L_DEV = 1024
SEQ = 4096


def draw_queries(key, part):
    own_key = jax.random.fold_in(key, 23)
    drawn = jnp.clip(2.5 * jax.random.normal(own_key, (SEQ, KVH, GQA, DH), jnp.float32), -10.0, 10.0)
    return drawn.astype(jnp.bfloat16)


def draw_keys_values(key, part):
    own_key = jax.random.fold_in(key, 29)
    drawn = jnp.clip(jax.random.normal(own_key, (2, SEQ, KVH, DH), jnp.float32), -6.0, 6.0)
    return drawn.astype(jnp.bfloat16)


def far_tables(key):
    base_key = jax.random.fold_in(key, 5)
    pool_key, order_key, jitter_key, filler_key = jax.random.split(base_key, 4)
    span_blocks = L_DEV // BLK
    span_total = SEQ // L_DEV
    all_blocks = span_blocks * span_total
    local_ids = jnp.arange(span_blocks, dtype=jnp.int32)
    span_ids = jnp.arange(span_total, dtype=jnp.int32)
    raw_scores = jax.random.randint(pool_key, (span_total, span_total, span_blocks), 0, 1 << 20, dtype=jnp.int32)
    too_late = (span_ids[None, :, None] == span_ids[:, None, None]) & (local_ids[None, None, :] >= span_blocks - WB)
    pool_score = raw_scores * span_blocks + local_ids[None, None, :] + too_late.astype(jnp.int32) * (1 << 26)
    pool_order = jnp.argsort(pool_score, axis=-1)[:, :, :CAP].astype(jnp.int32)
    pool_blocks = pool_order + span_ids[None, :, None] * span_blocks
    pool_ok = jnp.broadcast_to(span_ids[None, :, None] <= span_ids[:, None, None], pool_blocks.shape)
    block_ids = jnp.arange(all_blocks, dtype=jnp.int32)
    span_of = block_ids // span_blocks
    pool_width = span_total * CAP
    candidates = pool_blocks[span_of].reshape(all_blocks, pool_width)
    eligible = pool_ok[span_of].reshape(all_blocks, pool_width) & (candidates <= block_ids[:, None] - WB)
    owner_draw = jax.random.randint(order_key, (all_blocks, span_total), 0, 1 << 20, dtype=jnp.int32) * span_total + span_ids[None, :]
    owner_rank = jnp.argsort(jnp.argsort(owner_draw, axis=1), axis=1).astype(jnp.int32)
    slot_key = (owner_rank[:, :, None] * CAP + jnp.arange(CAP, dtype=jnp.int32)[None, None, :]).reshape(all_blocks, pool_width)
    sort_key = jnp.where(eligible, slot_key, slot_key + pool_width)
    picked = jnp.argsort(sort_key, axis=1)
    listed = jnp.take_along_axis(candidates, picked, axis=1).astype(jnp.int32)
    available = jnp.sum(eligible.astype(jnp.int32), axis=1)
    jitter = jax.random.randint(jitter_key, (all_blocks,), 0, 2, dtype=jnp.int32)
    jitter = jnp.where(block_ids == all_blocks - 1, 0, jitter)
    target = FSEL * (span_of + 1) // span_total - jitter
    counts = jnp.clip(jnp.minimum(target, available), 0, FSEL).astype(jnp.int32)
    if pool_width >= FSEL:
        listed = listed[:, :FSEL]
    else:
        listed = jnp.concatenate([listed, jnp.zeros((all_blocks, FSEL - pool_width), jnp.int32)], axis=1)
    filler = jax.random.randint(filler_key, (all_blocks, FSEL), 0, all_blocks, dtype=jnp.int32)
    listed = jnp.where(jnp.arange(FSEL, dtype=jnp.int32)[None, :] < counts[:, None], listed, filler)
    return (listed, counts)


def draw_far_list(key, part):
    return far_tables(key)[0]


def draw_far_count(key, part):
    return far_tables(key)[1]


def setup_inputs(seed: int = 0, part: int = 0) -> dict:
    streams_of = jax.random.split(jax.random.key(seed), 5)
    part_splits = jax.random.split(jax.random.fold_in(streams_of[4], part), 5)
    return {
        "queries": draw_queries(jax.random.fold_in(jax.random.fold_in(streams_of[4], part), 71), part),
        "keys_values": draw_keys_values(jax.random.fold_in(jax.random.fold_in(streams_of[4], part), 71), part),
        "far_list": draw_far_list(jax.random.fold_in(jax.random.fold_in(streams_of[4], part), 71), part),
        "far_count": draw_far_count(jax.random.fold_in(jax.random.fold_in(streams_of[4], part), 71), part),
    }


floor_score = -1.0e30
score_scale = 1.0 / 12.0


def group_weights(scores, usable):
    masked = jnp.where(usable, scores, floor_score)
    summit = jnp.max(masked, axis=-1, keepdims=True)
    weights = jnp.where(usable, jnp.exp(masked - summit), 0.0)
    return summit, weights, jnp.sum(weights, axis=-1, keepdims=True)


def attend(query_tile, keys_tile, values_tile, usable):
    scores = jnp.einsum("qhgd,khd->hgqk", query_tile.astype(jnp.float32), keys_tile.astype(jnp.float32), precision=lax.Precision.HIGHEST) * score_scale
    summit, weights, weight_sum = group_weights(scores, usable)
    light_weights = lax.optimization_barrier(weights.astype(jnp.bfloat16)).astype(jnp.float32)
    mixed_out = jnp.einsum("hgqk,khd->hgqd", light_weights, values_tile.astype(jnp.float32), precision=lax.Precision.HIGHEST)
    return summit, mixed_out, weight_sum


def reference(queries, keys_values, far_list, far_count):
    all_blocks = SEQ // BLK
    query_blocks = queries.reshape(all_blocks, BLK, KVH, GQA, DH)
    key_blocks = keys_values[0].reshape(all_blocks, BLK, KVH, DH)
    value_blocks = keys_values[1].reshape(all_blocks, BLK, KVH, DH)
    inside = jnp.arange(BLK, dtype=jnp.int32)
    window_pos = (jnp.arange(WB, dtype=jnp.int32)[:, None] * BLK + inside[None, :]).reshape(-1)
    slot_range = jnp.arange(FSEL, dtype=jnp.int32)

    def one_block(block_id):
        query_tile = query_blocks[block_id]
        window_ids = block_id - WB + 1 + jnp.arange(WB, dtype=jnp.int32)
        window_ok = jnp.repeat(window_ids >= 0, BLK)
        clipped = jnp.maximum(window_ids, 0).astype(jnp.int32)
        near_keys = key_blocks[clipped].reshape(WB * BLK, KVH, DH)
        near_values = value_blocks[clipped].reshape(WB * BLK, KVH, DH)
        query_pos = (WB - 1) * BLK + inside
        near_usable = (window_pos[None, :] <= query_pos[:, None]) & window_ok[None, :]
        near_top, near_out, near_sum = attend(query_tile, near_keys, near_values, near_usable)
        picked = far_list[block_id].astype(jnp.int32)
        far_keys = key_blocks[picked].reshape(FSEL * BLK, KVH, DH)
        far_values = value_blocks[picked].reshape(FSEL * BLK, KVH, DH)
        far_usable = jnp.repeat(slot_range < far_count[block_id], BLK)[None, :]
        far_top, far_out, far_sum = attend(query_tile, far_keys, far_values, far_usable)
        summit = jnp.maximum(near_top, far_top)
        near_scale = jnp.exp(near_top - summit)
        far_scale = jnp.exp(far_top - summit)
        result = (near_scale * near_out + far_scale * far_out) / (near_scale * near_sum + far_scale * far_sum)
        return jnp.transpose(result, (2, 0, 1, 3)).astype(jnp.bfloat16)

    outputs = lax.map(one_block, jnp.arange(all_blocks, dtype=jnp.int32))
    return outputs.reshape(SEQ, KVH, GQA, DH)
```

```python
import functools
import math

import jax
import jax.numpy as jnp
from jax import lax
from jax.experimental import pallas as pl
from jax.experimental.pallas import tpu as pltpu
from jax.sharding import PartitionSpec as P

BLK = 128
WB = 4
FSEL = 16
CAP = 2

LANES = 128
MASKED = -1e30
SCALE = math.log2(math.e) / 12.0
NT = (((1,), (1,)), ((), ()))


def kernel(
    spans, listed, q_in, kv_in, out,
    q_raw, mine, loc, rim, far, sendbuf, qh, kh, vh, tk, tv, acc, top, bias, scr, o_raw,
    in_sem, x_send, x_recv, rz_send, rz_recv, rf_send, rf_recv,
    fz_send, fz_recv, ff_send, ff_recv, out_sem,
):
    toks, heads, dh = q_in.shape
    own = toks // BLK
    me = lax.axis_index("ctx")
    side = lax.axis_index("rep")
    mate = {"rep": 1 - side}
    rims = WB - 1

    load_kv = pltpu.make_async_copy(kv_in.at[0], mine, in_sem.at[0])
    load_loc = pltpu.make_async_copy(kv_in.at[0], loc.at[side], in_sem.at[2])
    load_q = pltpu.make_async_copy(q_in, q_raw, in_sem.at[1])
    load_kv.start()
    load_q.start()
    load_loc.start()

    barrier = pltpu.get_barrier_semaphore()
    pl.semaphore_signal(barrier, inc=1, device_id=mate)

    def greet(i, _):
        pl.semaphore_signal(barrier, inc=1, device_id={"ctx": lax.rem(me + i, spans)})
        return 0

    lax.fori_loop(1, spans, greet, 0)
    pl.semaphore_wait(barrier, spans)

    def rim_copy(j, to):
        return pltpu.make_async_remote_copy(
            src_ref=kv_in.at[0, own - j],
            dst_ref=rim.at[side, j - 1],
            send_sem=rz_send.at[j - 1], recv_sem=rz_recv.at[j - 1],
            device_id={"ctx": to},
        )

    def rim_pass(j):
        return pltpu.make_async_remote_copy(
            src_ref=rim.at[side, j - 1], dst_ref=rim.at[side, j - 1],
            send_sem=rf_send.at[j - 1], recv_sem=rf_recv.at[j - 1],
            device_id=mate,
        )

    def far_copy(to):
        return pltpu.make_async_remote_copy(
            src_ref=sendbuf.at[to], dst_ref=far.at[side, me],
            send_sem=fz_send.at[to], recv_sem=fz_recv.at[me],
            device_id={"ctx": to},
        )

    def far_arrival(src):
        return pltpu.make_async_remote_copy(
            src_ref=sendbuf.at[src], dst_ref=far.at[side, src],
            send_sem=fz_send.at[src], recv_sem=fz_recv.at[src],
            device_id={"ctx": src},
        )

    def far_pass(src):
        return pltpu.make_async_remote_copy(
            src_ref=far.at[side, src], dst_ref=far.at[side, src],
            send_sem=ff_send.at[src], recv_sem=ff_recv.at[src],
            device_id=mate,
        )

    ahead = lax.rem(me + 1, spans)
    has_next = me + 1 < spans

    @pl.when(has_next)
    def _():
        rim_copy(1, ahead).start()

    swap = pltpu.make_async_remote_copy(
        src_ref=kv_in.at[0], dst_ref=loc.at[side],
        send_sem=x_send, recv_sem=x_recv, device_id=mate,
    )
    swap.start()

    big = jnp.int32(1 << 30)

    def slots(dst, src):
        lists = listed[pl.ds(pl.multiple_of(dst * own, own), own), :]
        inside = (lists >= src * own) & (lists < src * own + own)
        first = jnp.min(jnp.where(inside, lists, big))
        second = jnp.min(jnp.where(inside & (lists > first), lists, big))
        return lists, (first, second)

    def local_row(block):
        row = jnp.where(block < big, block - me * own, 0)
        return jnp.clip(row, 0, own - 1)

    load_kv.wait()

    def fill(i, _):
        to = spans - 1 - i
        _, found = slots(to, me)
        for k in range(CAP):
            sendbuf[to, k] = mine[local_row(found[k])]
        return 0

    later = spans - 1 - me
    lax.fori_loop(0, later, fill, 0)

    def push(i, _):
        far_copy(spans - 1 - i).start()
        return 0

    lax.fori_loop(0, later, push, 0)

    @pl.when(has_next)
    def _():
        for j in range(2, WB):
            rim_copy(j, ahead).start()

    def spread(block, put):
        scr[...] = block.astype(jnp.float32).reshape(BLK * heads, dh)
        for h in range(heads):
            put(h, scr[pl.ds(h, BLK, stride=heads), :].astype(jnp.bfloat16))

    tv[:, :, dh:] = jnp.ones((heads, CAP * BLK, LANES), jnp.bfloat16)
    vh[:, :, dh:] = jnp.ones((heads, toks, LANES), jnp.bfloat16)

    def fill_bias(src, _):
        lists, found = slots(me, src)
        for k in range(CAP):
            hit = jnp.max(jnp.where(lists == found[k], 1, 0), axis=1, keepdims=True)
            bias[src, :, k * BLK:(k + 1) * BLK] = jnp.broadcast_to(
                jnp.where(hit > 0, 0.0, MASKED), (own, BLK))
        return 0

    lax.fori_loop(0, me + 1, fill_bias, 0)

    load_q.wait()

    def spread_q(b, _):
        at = pl.ds(pl.multiple_of(b * BLK, BLK), BLK)

        def put(h, x):
            qh[h, at, :] = x

        spread(q_raw[at], put)
        return 0

    lax.fori_loop(0, own, spread_q, 0)
    load_loc.wait()
    swap.wait_recv()

    def spread_kv(b, _):
        at = pl.ds(pl.multiple_of(b * BLK, BLK), BLK)

        def put_k(h, x):
            kh[h, at, :] = x

        def put_v(h, x):
            vh[h, at, :dh] = x

        spread(loc[0, b], put_k)
        spread(loc[1, b], put_v)
        return 0

    lax.fori_loop(0, own, spread_kv, 0)

    span = min(WB * BLK, toks)

    def near(c, _):
        rows = pl.ds(pl.multiple_of(c * BLK, BLK), BLK)
        low = pl.multiple_of(jnp.maximum(c - (WB - 1), 0) * BLK, BLK)
        keys = pl.ds(low, span)
        key_pos = low + lax.broadcasted_iota(jnp.int32, (BLK, span), 1)
        query_pos = c * BLK + lax.broadcasted_iota(jnp.int32, (BLK, span), 0)
        seen = key_pos <= query_pos
        for h in range(heads):
            s = lax.dot_general(qh[h, rows, :], kh[h, keys, :], NT,
                                preferred_element_type=jnp.float32) * SCALE
            s = jnp.where(seen, s, MASKED)
            m = jnp.max(s, axis=1, keepdims=True)
            p = jnp.exp2(s - m).astype(jnp.bfloat16)
            acc[h, rows, :] = jnp.dot(p, vh[h, keys, :], preferred_element_type=jnp.float32)
            top[h, rows, :] = jnp.broadcast_to(m, (BLK, LANES))
        return 0

    lax.fori_loop(0, own, near, 0)

    def merge(h, rows, k, v, row_bias):
        s = lax.dot_general(qh[h, rows, :], k, NT, preferred_element_type=jnp.float32) * SCALE
        if row_bias is not None:
            s = s + row_bias
        old = top[h, rows, :]
        m = jnp.maximum(old, jnp.max(s, axis=1, keepdims=True))
        wide = jnp.concatenate([m] * (s.shape[1] // LANES), axis=1)
        p = jnp.exp2(s - wide).astype(jnp.bfloat16)
        a = jnp.exp2(old - m)
        acc[h, rows, :] = acc[h, rows, :] * jnp.concatenate([a, a], axis=1) + jnp.dot(
            p, v, preferred_element_type=jnp.float32)
        top[h, rows, :] = m

    def spread_pair(get):
        for k in range(CAP):
            at = slice(k * BLK, (k + 1) * BLK)

            def put_k(h, x):
                tk[h, at, :] = x

            def put_v(h, x):
                tv[h, at, :dh] = x

            spread(get(0, k), put_k)
            spread(get(1, k), put_v)

    def far_all(src):
        def one(c, _):
            rows = pl.ds(pl.multiple_of(c * BLK, BLK), BLK)
            row_bias = bias[src, pl.ds(c, 1), :]
            for h in range(heads):
                merge(h, rows, tk[h], tv[h], row_bias)
            return 0

        lax.fori_loop(0, own, one, 0)

    _, found = slots(me, me)
    at_mine = [local_row(b) for b in found]
    spread_pair(lambda kind, k: loc[kind, at_mine[k]])
    far_all(me)

    @pl.when(me > 0)
    def _():
        rim_copy(1, ahead).wait_recv()
        rim_pass(1).start()

    def far_step(i, _):
        src = me - 1 - i
        far_arrival(src).wait_recv()
        far_pass(src).start()
        far_pass(src).wait_recv()
        spread_pair(lambda kind, k: far[kind, src, k])
        far_all(src)
        return 0

    lax.fori_loop(0, me, far_step, 0)

    def finish(c, _):
        rows = pl.ds(pl.multiple_of(c * BLK, BLK), BLK)
        for h in range(heads):
            scr[pl.ds(h, BLK, stride=heads), :] = acc[h, rows, :dh] / acc[h, rows, dh:]
        o_raw[rows] = scr[...].reshape(BLK, heads, dh).astype(jnp.bfloat16)
        pltpu.make_async_copy(o_raw.at[rows], out.at[rows], out_sem.at[c]).start()
        return 0

    lax.fori_loop(min(rims, own), own, finish, 0)

    for j in range(1, WB):
        @pl.when(me > 0)
        def _():
            if j > 1:
                rim_copy(j, ahead).wait_recv()
                rim_pass(j).start()
            rim_pass(j).wait_recv()

            def put_k(h, x):
                tk[h, :BLK, :] = x

            def put_v(h, x):
                tv[h, :BLK, :dh] = x

            spread(rim[0, j - 1], put_k)
            spread(rim[1, j - 1], put_v)

            def one(c, _):
                rows = pl.ds(pl.multiple_of(c * BLK, BLK), BLK)
                for h in range(heads):
                    merge(h, rows, tk[h, :BLK, :], tv[h, :BLK, :], None)
                return 0

            lax.fori_loop(0, min(WB - j, own), one, 0)

        if WB - j - 1 < own:
            finish(WB - j - 1, 0)

    def drain(c, _):
        rows = pl.ds(pl.multiple_of(c * BLK, BLK), BLK)
        pltpu.make_async_copy(o_raw.at[rows], out.at[rows], out_sem.at[c]).wait()
        return 0

    lax.fori_loop(0, own, drain, 0)
    swap.wait_send()

    @pl.when(has_next)
    def _():
        for j in range(1, WB):
            rim_copy(j, ahead).wait_send()

    @pl.when(me > 0)
    def _():
        for j in range(1, WB):
            rim_pass(j).wait_send()

    def sent(i, _):
        far_copy(spans - 1 - i).wait_send()
        return 0

    lax.fori_loop(0, later, sent, 0)

    def passed(src, _):
        far_pass(src).wait_send()
        return 0

    lax.fori_loop(0, me, passed, 0)


def local(spans, queries, keys_values, far_list, far_count):
    toks, heads, members, dh = queries.shape
    own = toks // BLK
    rims = WB - 1
    slot = jnp.arange(far_list.shape[1], dtype=jnp.int32)
    listed = jnp.where(slot[None, :] < far_count[:, None], far_list, -1)
    bf16, f32 = jnp.bfloat16, jnp.float32
    hbm = pl.BlockSpec(memory_space=pl.ANY)
    dma = pltpu.SemaphoreType.DMA
    result = pl.pallas_call(
        functools.partial(kernel, spans),
        out_shape=jax.ShapeDtypeStruct((toks, heads, dh), bf16),
        in_specs=[pl.BlockSpec(memory_space=pltpu.VMEM), hbm, hbm],
        out_specs=hbm,
        scratch_shapes=[
            pltpu.VMEM((toks, heads, dh), bf16),
            pltpu.VMEM((own, BLK, heads, dh), bf16),
            pltpu.VMEM((2, own, BLK, heads, dh), bf16),
            pltpu.VMEM((2, rims, BLK, heads, dh), bf16),
            pltpu.VMEM((2, spans, CAP, BLK, heads, dh), bf16),
            pltpu.VMEM((spans, CAP, BLK, heads, dh), bf16),
            pltpu.VMEM((heads, toks, dh), bf16),
            pltpu.VMEM((heads, toks, dh), bf16),
            pltpu.VMEM((heads, toks, dh + LANES), bf16),
            pltpu.VMEM((heads, CAP * BLK, dh), bf16),
            pltpu.VMEM((heads, CAP * BLK, dh + LANES), bf16),
            pltpu.VMEM((heads, toks, dh + LANES), f32),
            pltpu.VMEM((heads, toks, LANES), f32),
            pltpu.VMEM((spans, own, CAP * BLK), f32),
            pltpu.VMEM((BLK * heads, dh), f32),
            pltpu.VMEM((toks, heads, dh), bf16),
            dma((3,)), dma, dma,
            dma((rims,)), dma((rims,)), dma((rims,)), dma((rims,)),
            dma((spans,)), dma((spans,)), dma((spans,)), dma((spans,)),
            dma((own,)),
        ],
        compiler_params=pltpu.CompilerParams(
            collective_id=0, has_side_effects=True, vmem_limit_bytes=62 << 20),
    )(listed, queries.reshape(toks, heads, dh), keys_values.reshape(-1, own, BLK, heads, dh))
    return result.reshape(queries.shape)


def solution(mesh):
    in_specs = (
        P(("groups", "ctx"), "head", "rep", None),
        P("rep", ("groups", "ctx"), "head", None),
        P("groups", None),
        P("groups"),
    )
    out_specs = P(("groups", "ctx"), "head", "rep", None)
    return jax.shard_map(
        functools.partial(local, mesh.shape["ctx"]),
        mesh=mesh, in_specs=in_specs, out_specs=out_specs, check_vma=False)
```

```python
import functools
import math

import jax
import jax.numpy as jnp
from jax import lax
from jax.experimental import pallas as pl
from jax.experimental.pallas import tpu as pltpu
from jax.sharding import PartitionSpec as P

BLK = 128
WB = 4
FSEL = 16
CAP = 2

LANES = 128
MASKED = -1e30
SCALE = math.log2(math.e) / 12.0
NT = (((1,), (1,)), ((), ()))


def kernel(
    spans, lists_in, counts, q_in, kv_in, out,
    q_raw, raw, mine, loc, rim_raw, rim, far, sendbuf, qh, tk, tv, acc, top, bias, scr, o_raw,
    in_sem, x_send, x_recv, rz_send, rz_recv, rf_send, rf_recv,
    fz_send, fz_recv, ff_send, ff_recv, out_sem,
):
    toks, heads, dh = q_in.shape
    own = toks // BLK
    me = lax.axis_index("ctx")
    side = lax.axis_index("rep")
    mate = {"rep": 1 - side}
    rims = WB - 1

    load_kv = pltpu.make_async_copy(kv_in.at[0], raw, in_sem.at[0])
    load_q = pltpu.make_async_copy(q_in, q_raw, in_sem.at[1])
    load_kv.start()
    load_q.start()

    barrier = pltpu.get_barrier_semaphore()
    pl.semaphore_signal(barrier, inc=1, device_id=mate)

    def greet(i, _):
        pl.semaphore_signal(barrier, inc=1, device_id={"ctx": lax.rem(me + i, spans)})
        return 0

    lax.fori_loop(1, spans, greet, 0)
    pl.semaphore_wait(barrier, spans)

    def rim_copy(j, to):
        return pltpu.make_async_remote_copy(
            src_ref=kv_in.at[0, own - j] if j == 1 else mine.at[own - j],
            dst_ref=rim_raw.at[side] if j == 1 else rim.at[side, j - 2],
            send_sem=rz_send.at[j - 1], recv_sem=rz_recv.at[j - 1],
            device_id={"ctx": to},
        )

    def rim_pass(j):
        return pltpu.make_async_remote_copy(
            src_ref=rim_raw.at[side] if j == 1 else rim.at[side, j - 2],
            dst_ref=rim_raw.at[side] if j == 1 else rim.at[side, j - 2],
            send_sem=rf_send.at[j - 1], recv_sem=rf_recv.at[j - 1],
            device_id=mate,
        )

    def far_copy(to):
        return pltpu.make_async_remote_copy(
            src_ref=sendbuf.at[to], dst_ref=far.at[side, me],
            send_sem=fz_send.at[to], recv_sem=fz_recv.at[me],
            device_id={"ctx": to},
        )

    def far_arrival(src):
        return pltpu.make_async_remote_copy(
            src_ref=sendbuf.at[src], dst_ref=far.at[side, src],
            send_sem=fz_send.at[src], recv_sem=fz_recv.at[src],
            device_id={"ctx": src},
        )

    def far_pass(src):
        return pltpu.make_async_remote_copy(
            src_ref=far.at[side, src], dst_ref=far.at[side, src],
            send_sem=ff_send.at[src], recv_sem=ff_recv.at[src],
            device_id=mate,
        )

    ahead = lax.rem(me + 1, spans)
    has_next = me + 1 < spans

    @pl.when(has_next)
    def _():
        rim_copy(1, ahead).start()

    def spread(part, block, put):
        scr[part] = block.astype(jnp.float32).reshape(BLK * heads, dh)
        for h in range(heads):
            put(h, scr[part, pl.ds(h, BLK, stride=heads), :].astype(jnp.bfloat16))

    load_kv.wait()
    parts = scr.shape[0]

    def spread_mine(i, _):
        for part in range(parts):
            b = i * parts + part

            def put(h, x):
                mine[b, h] = x
                loc[side, b, h] = x

            spread(part, raw[b], put)
        return 0

    lax.fori_loop(0, own // parts, spread_mine, 0)

    swap = pltpu.make_async_remote_copy(
        src_ref=mine, dst_ref=loc.at[side],
        send_sem=x_send, recv_sem=x_recv, device_id=mate,
    )
    swap.start()

    big = jnp.int32(1 << 30)
    slot = lax.broadcasted_iota(jnp.int32, lists_in.shape, 0)
    block_of = lax.broadcasted_iota(jnp.int32, lists_in.shape, 1)
    listed = jnp.where(slot < counts[...], lists_in[...], -1)

    def slots(dst, src):
        inside = ((listed >= src * own) & (listed < src * own + own)
                  & (block_of >= dst * own) & (block_of < dst * own + own))
        first = jnp.min(jnp.where(inside, listed, big))
        second = jnp.min(jnp.where(inside & (listed > first), listed, big))
        return first, second

    def local_row(block):
        row = jnp.where(block < big, block - me * own, 0)
        return jnp.clip(row, 0, own - 1)

    def fill(i, _):
        to = spans - 1 - i
        found = slots(to, me)
        for k in range(CAP):
            sendbuf[to, k] = mine[local_row(found[k])]
        return 0

    later = spans - 1 - me
    lax.fori_loop(0, later, fill, 0)

    def push(i, _):
        far_copy(spans - 1 - i).start()
        return 0

    lax.fori_loop(0, later, push, 0)

    @pl.when(has_next)
    def _():
        for j in range(2, WB):
            rim_copy(j, ahead).start()

    ones = jnp.ones((BLK, LANES), jnp.bfloat16)

    def fill_bias(src, _):
        found = slots(me, src)
        for k in range(CAP):
            hit = jnp.max(jnp.where(listed == found[k], 1.0, 0.0), axis=0, keepdims=True)
            for c in range(own):
                mark = jnp.where(block_of[:1] == me * own + c, hit, 0.0)
                mark = jnp.max(mark, axis=1, keepdims=True)
                bias[src, c, :, k * BLK:(k + 1) * BLK] = jnp.broadcast_to(
                    jnp.where(mark > 0.5, 0.0, MASKED), (1, BLK))
        return 0

    lax.fori_loop(0, me + 1, fill_bias, 0)

    load_q.wait()

    def spread_q(i, _):
        for part in range(parts):
            at = pl.ds(pl.multiple_of((i * parts + part) * BLK, BLK), BLK)

            def put(h, x):
                qh[h, at, :] = x

            spread(part, q_raw[at], put)
        return 0

    lax.fori_loop(0, own // parts, spread_q, 0)
    swap.wait_recv()

    wide = min(WB, own)
    span = wide * BLK

    def near(c, _):
        rows = pl.ds(pl.multiple_of(c * BLK, BLK), BLK)
        low = jnp.maximum(c - (WB - 1), 0)
        keys = pl.ds(low, wide)
        key_pos = low * BLK + lax.broadcasted_iota(jnp.int32, (BLK, span), 1)
        query_pos = c * BLK + lax.broadcasted_iota(jnp.int32, (BLK, span), 0)
        seen = key_pos <= query_pos
        for h in range(heads):
            s = lax.dot_general(qh[h, rows, :], loc[0, keys, h].reshape(span, dh), NT,
                                preferred_element_type=jnp.float32) * SCALE
            s = jnp.where(seen, s, MASKED)
            m = jnp.max(s, axis=1, keepdims=True)
            p = jnp.exp2(s - m).astype(jnp.bfloat16)
            v = jnp.concatenate([loc[1, keys, h].reshape(span, dh)] + [jnp.ones((span, LANES), jnp.bfloat16)], axis=1)
            acc[h, rows, :] = jnp.dot(p, v, preferred_element_type=jnp.float32)
            top[h, rows, :] = jnp.broadcast_to(m, (BLK, LANES))
        return 0

    lax.fori_loop(0, own, near, 0)

    def merge(h, rows, k, v, row_bias):
        s = lax.dot_general(qh[h, rows, :], k, NT, preferred_element_type=jnp.float32) * SCALE
        if row_bias is not None:
            s = s + row_bias
        old = top[h, rows, :]
        m = jnp.maximum(old, jnp.max(s, axis=1, keepdims=True))
        spread_m = jnp.concatenate([m] * (s.shape[1] // LANES), axis=1)
        p = jnp.exp2(s - spread_m).astype(jnp.bfloat16)
        a = jnp.exp2(old - m)
        acc[h, rows, :] = acc[h, rows, :] * jnp.concatenate([a, a], axis=1) + jnp.dot(
            p, v, preferred_element_type=jnp.float32)
        top[h, rows, :] = m

    def stack(get, h):
        k = jnp.concatenate([get(0, n, h) for n in range(CAP)], axis=0)
        v = jnp.concatenate(
            [jnp.concatenate([get(1, n, h), ones], axis=1) for n in range(CAP)], axis=0)
        return k, v

    def far_all(src, get):
        def one(c, _):
            rows = pl.ds(pl.multiple_of(c * BLK, BLK), BLK)
            row_bias = bias[src, c]
            for h in range(heads):
                merge(h, rows, *stack(get, h), row_bias)
            return 0

        lax.fori_loop(0, own, one, 0)

    found_mine = slots(me, me)
    at_mine = [local_row(b) for b in found_mine]
    far_all(me, lambda kind, k, h: loc[kind, at_mine[k], h])

    def rim_all(j, get):
        def one(c, _):
            rows = pl.ds(pl.multiple_of(c * BLK, BLK), BLK)
            for h in range(heads):
                merge(h, rows, get(0, h), jnp.concatenate([get(1, h), ones], axis=1), None)
            return 0

        lax.fori_loop(0, min(WB - j, own), one, 0)

    @pl.when(me > 0)
    def _():
        rim_copy(1, ahead).wait_recv()
        rim_pass(1).start()
        rim_pass(1).wait_recv()

        def put_k(h, x):
            tk[h] = x

        def put_v(h, x):
            tv[h] = x

        spread(0, rim_raw[0], put_k)
        spread(1, rim_raw[1], put_v)
        rim_all(1, lambda kind, h: (tv if kind else tk)[h])

    def far_step(src, _):
        far_arrival(src).wait_recv()
        far_pass(src).start()
        far_pass(src).wait_recv()
        far_all(src, lambda kind, k, h: far[kind, src, k, h])
        return 0

    lax.fori_loop(0, me, far_step, 0)

    def finish(c, _):
        rows = pl.ds(pl.multiple_of(c * BLK, BLK), BLK)
        part = lax.rem(c, parts)
        for h in range(heads):
            scr[part, pl.ds(h, BLK, stride=heads), :] = acc[h, rows, :dh] / acc[h, rows, dh:]
        o_raw[rows] = scr[part].reshape(BLK, heads, dh).astype(jnp.bfloat16)
        pltpu.make_async_copy(o_raw.at[rows], out.at[rows], out_sem.at[c]).start()
        return 0

    lax.fori_loop(min(rims - 1, own), own, finish, 0)

    for j in range(2, WB):
        @pl.when(me > 0)
        def _():
            rim_copy(j, ahead).wait_recv()
            rim_pass(j).start()
            rim_pass(j).wait_recv()
            rim_all(j, lambda kind, h: rim[kind, j - 2, h])

        if WB - j - 1 < own:
            finish(WB - j - 1, 0)

    def drain(c, _):
        rows = pl.ds(pl.multiple_of(c * BLK, BLK), BLK)
        pltpu.make_async_copy(o_raw.at[rows], out.at[rows], out_sem.at[c]).wait()
        return 0

    lax.fori_loop(0, own, drain, 0)
    swap.wait_send()

    @pl.when(has_next)
    def _():
        for j in range(1, WB):
            rim_copy(j, ahead).wait_send()

    @pl.when(me > 0)
    def _():
        for j in range(1, WB):
            rim_pass(j).wait_send()

    def sent(i, _):
        far_copy(spans - 1 - i).wait_send()
        return 0

    lax.fori_loop(0, later, sent, 0)

    def passed(src, _):
        far_pass(src).wait_send()
        return 0

    lax.fori_loop(0, me, passed, 0)


def local(spans, queries, keys_values, far_list, far_count):
    toks, heads, members, dh = queries.shape
    own = toks // BLK
    rims = WB - 1
    bf16, f32 = jnp.bfloat16, jnp.float32
    hbm = pl.BlockSpec(memory_space=pl.ANY)
    dma = pltpu.SemaphoreType.DMA
    result = pl.pallas_call(
        functools.partial(kernel, spans),
        out_shape=jax.ShapeDtypeStruct((toks, heads, dh), bf16),
        in_specs=[pl.BlockSpec(memory_space=pltpu.VMEM)] * 2 + [hbm, hbm],
        out_specs=hbm,
        scratch_shapes=[
            pltpu.VMEM((toks, heads, dh), bf16),
            pltpu.VMEM((own, BLK, heads, dh), bf16),
            pltpu.VMEM((own, heads, BLK, dh), bf16),
            pltpu.VMEM((2, own, heads, BLK, dh), bf16),
            pltpu.VMEM((2, BLK, heads, dh), bf16),
            pltpu.VMEM((2, rims - 1, heads, BLK, dh), bf16),
            pltpu.VMEM((2, spans, CAP, heads, BLK, dh), bf16),
            pltpu.VMEM((spans, CAP, heads, BLK, dh), bf16),
            pltpu.VMEM((heads, toks, dh), bf16),
            pltpu.VMEM((heads, BLK, dh), bf16),
            pltpu.VMEM((heads, BLK, dh), bf16),
            pltpu.VMEM((heads, toks, dh + LANES), f32),
            pltpu.VMEM((heads, toks, LANES), f32),
            pltpu.VMEM((spans, own, 1, CAP * BLK), f32),
            pltpu.VMEM((2, BLK * heads, dh), f32),
            pltpu.VMEM((toks, heads, dh), bf16),
            dma((2,)), dma, dma,
            dma((rims,)), dma((rims,)), dma((rims,)), dma((rims,)),
            dma((spans,)), dma((spans,)), dma((spans,)), dma((spans,)),
            dma((own,)),
        ],
        compiler_params=pltpu.CompilerParams(
            collective_id=0, has_side_effects=True, vmem_limit_bytes=62 << 20),
    )(far_list.T, far_count.reshape(1, -1), queries.reshape(toks, heads, dh), keys_values.reshape(-1, own, BLK, heads, dh))
    return result.reshape(queries.shape)


def solution(mesh):
    in_specs = (
        P(("groups", "ctx"), "head", "rep", None),
        P("rep", ("groups", "ctx"), "head", None),
        P("groups", None),
        P("groups"),
    )
    out_specs = P(("groups", "ctx"), "head", "rep", None)
    return jax.shard_map(
        functools.partial(local, mesh.shape["ctx"]),
        mesh=mesh, in_specs=in_specs, out_specs=out_specs, check_vma=False)
```

```python
import functools
import math

import jax
import jax.numpy as jnp
from jax import lax
from jax.experimental import pallas as pl
from jax.experimental.pallas import tpu as pltpu
from jax.sharding import PartitionSpec as P

BLK = 128
WB = 4
FSEL = 16
CAP = 2

LANES = 128
MASKED = -1e30
SCALE = math.log2(math.e) / 12.0
NT = (((1,), (1,)), ((), ()))


def kernel(
    spans, lists_in, counts, q_in, kv_in, out,
    q_raw, raw, mine, loc, rim_raw, rim, far, sendbuf, qh, acc, top, bias, scr, o_raw,
    in_sem, x_send, x_recv, rz_send, rz_recv, rf_send, rf_recv,
    fz_send, fz_recv, ff_send, ff_recv, out_sem,
):
    toks, heads, dh = q_in.shape
    own = toks // BLK
    me = lax.axis_index("ctx")
    side = lax.axis_index("rep")
    mate = {"rep": 1 - side}
    rims = WB - 1

    load_kv = pltpu.make_async_copy(kv_in.at[0], raw, in_sem.at[0])
    load_q = pltpu.make_async_copy(q_in, q_raw, in_sem.at[1])
    load_kv.start()
    load_q.start()

    barrier = pltpu.get_barrier_semaphore()
    pl.semaphore_signal(barrier, inc=1, device_id=mate)

    def greet(i, _):
        pl.semaphore_signal(barrier, inc=1, device_id={"ctx": lax.rem(me + i, spans)})
        return 0

    lax.fori_loop(1, spans, greet, 0)
    pl.semaphore_wait(barrier, spans)

    def raw_copy(to):
        return pltpu.make_async_remote_copy(
            src_ref=kv_in.at[0, own - 1], dst_ref=rim_raw.at[side],
            send_sem=rz_send.at[0], recv_sem=rz_recv.at[0], device_id={"ctx": to},
        )

    def raw_pass():
        return pltpu.make_async_remote_copy(
            src_ref=rim_raw.at[side], dst_ref=rim_raw.at[side],
            send_sem=rf_send.at[0], recv_sem=rf_recv.at[0], device_id=mate,
        )

    def rim_copy(j, to):
        return pltpu.make_async_remote_copy(
            src_ref=mine.at[own - j],
            dst_ref=rim.at[side, j - 1],
            send_sem=rz_send.at[j - 1], recv_sem=rz_recv.at[j - 1],
            device_id={"ctx": to},
        )

    def rim_pass(j):
        return pltpu.make_async_remote_copy(
            src_ref=rim.at[side, j - 1],
            dst_ref=rim.at[side, j - 1],
            send_sem=rf_send.at[j - 1], recv_sem=rf_recv.at[j - 1],
            device_id=mate,
        )

    def far_copy(to):
        return pltpu.make_async_remote_copy(
            src_ref=sendbuf.at[to], dst_ref=far.at[side, me],
            send_sem=fz_send.at[to], recv_sem=fz_recv.at[me],
            device_id={"ctx": to},
        )

    def far_arrival(src):
        return pltpu.make_async_remote_copy(
            src_ref=sendbuf.at[src], dst_ref=far.at[side, src],
            send_sem=fz_send.at[src], recv_sem=fz_recv.at[src],
            device_id={"ctx": src},
        )

    def far_pass(src):
        return pltpu.make_async_remote_copy(
            src_ref=far.at[side, src], dst_ref=far.at[side, src],
            send_sem=ff_send.at[src], recv_sem=ff_recv.at[src],
            device_id=mate,
        )

    ahead = lax.rem(me + 1, spans)
    has_next = me + 1 < spans

    @pl.when(has_next)
    def _():
        raw_copy(ahead).start()

    def spread(part, block, put):
        scr[part] = block.astype(jnp.float32).reshape(BLK * heads, dh)
        for h in range(heads):
            put(h, scr[part, pl.ds(h, BLK, stride=heads), :].astype(jnp.bfloat16))

    load_kv.wait()
    parts = scr.shape[0]

    def spread_mine(i, _):
        for part in range(parts):
            b = i * parts + part

            def put(h, x):
                mine[b, h] = x
                loc[side, b, h] = x

            spread(part, raw[b], put)
        return 0

    lax.fori_loop(0, own // parts, spread_mine, 0)

    swap = pltpu.make_async_remote_copy(
        src_ref=mine, dst_ref=loc.at[side],
        send_sem=x_send, recv_sem=x_recv, device_id=mate,
    )
    swap.start()

    big = jnp.int32(1 << 30)
    slot = lax.broadcasted_iota(jnp.int32, lists_in.shape, 0)
    block_of = lax.broadcasted_iota(jnp.int32, lists_in.shape, 1)
    listed = jnp.where(slot < counts[...], lists_in[...], -1)

    def slots(dst, src):
        inside = ((listed >= src * own) & (listed < src * own + own)
                  & (block_of >= dst * own) & (block_of < dst * own + own))
        first = jnp.min(jnp.where(inside, listed, big))
        second = jnp.min(jnp.where(inside & (listed > first), listed, big))
        return first, second

    def local_row(block):
        row = jnp.where(block < big, block - me * own, 0)
        return jnp.clip(row, 0, own - 1)

    def fill(i, _):
        to = spans - 1 - i
        found = slots(to, me)
        for k in range(CAP):
            sendbuf[to, k] = mine[local_row(found[k])]
        return 0

    later = spans - 1 - me
    lax.fori_loop(0, later, fill, 0)

    def push(i, _):
        far_copy(spans - 1 - i).start()
        return 0

    lax.fori_loop(0, later, push, 0)

    @pl.when(has_next)
    def _():
        for j in range(2, WB):
            rim_copy(j, ahead).start()

    ones = jnp.ones((BLK, LANES), jnp.bfloat16)

    def fill_bias(src, _):
        found = slots(me, src)
        for k in range(CAP):
            hit = jnp.max(jnp.where(listed == found[k], 1.0, 0.0), axis=0, keepdims=True)
            for c in range(own):
                mark = jnp.where(block_of[:1] == me * own + c, hit, 0.0)
                mark = jnp.max(mark, axis=1, keepdims=True)
                bias[src, c, :, k * BLK:(k + 1) * BLK] = jnp.broadcast_to(
                    jnp.where(mark > 0.5, 0.0, MASKED), (1, BLK))
        return 0

    lax.fori_loop(0, me + 1, fill_bias, 0)

    load_q.wait()

    def spread_q(i, _):
        for part in range(parts):
            at = pl.ds(pl.multiple_of((i * parts + part) * BLK, BLK), BLK)

            def put(h, x):
                qh[h, at, :] = x

            spread(part, q_raw[at], put)
        return 0

    lax.fori_loop(0, own // parts, spread_q, 0)
    swap.wait_recv()

    wide = min(WB, own)
    span = wide * BLK

    def near(c, _):
        rows = pl.ds(pl.multiple_of(c * BLK, BLK), BLK)
        low = jnp.maximum(c - (WB - 1), 0)
        keys = pl.ds(low, wide)
        key_pos = low * BLK + lax.broadcasted_iota(jnp.int32, (BLK, span), 1)
        query_pos = c * BLK + lax.broadcasted_iota(jnp.int32, (BLK, span), 0)
        seen = key_pos <= query_pos
        for h in range(heads):
            s = lax.dot_general(qh[h, rows, :], loc[0, keys, h].reshape(span, dh), NT,
                                preferred_element_type=jnp.float32) * SCALE
            s = jnp.where(seen, s, MASKED)
            m = jnp.max(s, axis=1, keepdims=True)
            p = jnp.exp2(s - m).astype(jnp.bfloat16)
            v = jnp.concatenate([loc[1, keys, h].reshape(span, dh)] + [jnp.ones((span, LANES), jnp.bfloat16)], axis=1)
            acc[h, rows, :] = jnp.dot(p, v, preferred_element_type=jnp.float32)
            top[h, rows, :] = jnp.broadcast_to(m, (BLK, LANES))
        return 0

    lax.fori_loop(0, own, near, 0)

    def merge(h, rows, k, v, row_bias):
        s = lax.dot_general(qh[h, rows, :], k, NT, preferred_element_type=jnp.float32) * SCALE
        s = s + row_bias
        old = top[h, rows, :]
        m = jnp.maximum(old, jnp.max(s, axis=1, keepdims=True))
        spread_m = jnp.concatenate([m] * (s.shape[1] // LANES), axis=1)
        p = jnp.exp2(s - spread_m).astype(jnp.bfloat16)
        a = jnp.exp2(old - m)
        acc[h, rows, :] = acc[h, rows, :] * jnp.concatenate([a, a], axis=1) + jnp.dot(
            p, v, preferred_element_type=jnp.float32)
        top[h, rows, :] = m

    def stack(get, h):
        k = jnp.concatenate([get(0, n, h) for n in range(CAP)], axis=0)
        v = jnp.concatenate(
            [jnp.concatenate([get(1, n, h), ones], axis=1) for n in range(CAP)], axis=0)
        return k, v

    def far_all(src, get):
        def one(c, _):
            rows = pl.ds(pl.multiple_of(c * BLK, BLK), BLK)
            row_bias = bias[src, c]
            for h in range(heads):
                merge(h, rows, *stack(get, h), row_bias)
            return 0

        lax.fori_loop(0, own, one, 0)

    found_mine = slots(me, me)
    at_mine = [local_row(b) for b in found_mine]
    far_all(me, lambda kind, k, h: loc[kind, at_mine[k], h])

    @pl.when(me > 0)
    def _():
        raw_copy(ahead).wait_recv()
        raw_pass().start()
        raw_pass().wait_recv()

        def put_k(h, x):
            rim[0, 0, h] = x

        def put_v(h, x):
            rim[1, 0, h] = x

        spread(0, rim_raw[0], put_k)
        spread(1, rim_raw[1], put_v)

    def far_step(src, _):
        far_arrival(src).wait_recv()
        far_pass(src).start()
        far_pass(src).wait_recv()
        far_all(src, lambda kind, k, h: far[kind, src, k, h])
        return 0

    lax.fori_loop(0, me, far_step, 0)

    def finish(c, _):
        rows = pl.ds(pl.multiple_of(c * BLK, BLK), BLK)
        part = lax.rem(c, parts)
        for h in range(heads):
            scr[part, pl.ds(h, BLK, stride=heads), :] = acc[h, rows, :dh] / acc[h, rows, dh:]
        o_raw[rows] = scr[part].reshape(BLK, heads, dh).astype(jnp.bfloat16)
        pltpu.make_async_copy(o_raw.at[rows], out.at[rows], out_sem.at[c]).start()
        return 0

    lane = lax.broadcasted_iota(jnp.int32, (1, CAP * BLK), 1)
    once = jnp.where(lane < BLK, 0.0, MASKED)

    def close(i, _):
        last = own - 1 - i
        j = WB - 1 - last

        @pl.when((me > 0) & (j > 1))
        def _():
            rim_copy(j, ahead).wait_recv()
            rim_pass(j).start()
            rim_pass(j).wait_recv()

        def one(c, _):
            rows = pl.ds(pl.multiple_of(c * BLK, BLK), BLK)
            for h in range(heads):
                merge(h, rows, *stack(lambda kind, n, h: rim[kind, j - 1, h], h), once)
            return 0

        @pl.when((me > 0) & (j > 0))
        def _():
            lax.fori_loop(0, last + 1, one, 0)

        return finish(last, 0)

    lax.fori_loop(0, own, close, 0)

    def drain(c, _):
        rows = pl.ds(pl.multiple_of(c * BLK, BLK), BLK)
        pltpu.make_async_copy(o_raw.at[rows], out.at[rows], out_sem.at[c]).wait()
        return 0

    lax.fori_loop(0, own, drain, 0)
    swap.wait_send()

    @pl.when(has_next)
    def _():
        raw_copy(ahead).wait_send()
        for j in range(2, WB):
            rim_copy(j, ahead).wait_send()

    @pl.when(me > 0)
    def _():
        raw_pass().wait_send()
        for j in range(2, WB):
            rim_pass(j).wait_send()

    def sent(i, _):
        far_copy(spans - 1 - i).wait_send()
        return 0

    lax.fori_loop(0, later, sent, 0)

    def passed(src, _):
        far_pass(src).wait_send()
        return 0

    lax.fori_loop(0, me, passed, 0)


def local(spans, queries, keys_values, far_list, far_count):
    toks, heads, members, dh = queries.shape
    own = toks // BLK
    rims = WB - 1
    bf16, f32 = jnp.bfloat16, jnp.float32
    hbm = pl.BlockSpec(memory_space=pl.ANY)
    dma = pltpu.SemaphoreType.DMA
    result = pl.pallas_call(
        functools.partial(kernel, spans),
        out_shape=jax.ShapeDtypeStruct((toks, heads, dh), bf16),
        in_specs=[pl.BlockSpec(memory_space=pltpu.VMEM)] * 2 + [hbm, hbm],
        out_specs=hbm,
        scratch_shapes=[
            pltpu.VMEM((toks, heads, dh), bf16),
            pltpu.VMEM((own, BLK, heads, dh), bf16),
            pltpu.VMEM((own, heads, BLK, dh), bf16),
            pltpu.VMEM((2, own, heads, BLK, dh), bf16),
            pltpu.VMEM((2, BLK, heads, dh), bf16),
            pltpu.VMEM((2, rims, heads, BLK, dh), bf16),
            pltpu.VMEM((2, spans, CAP, heads, BLK, dh), bf16),
            pltpu.VMEM((spans, CAP, heads, BLK, dh), bf16),
            pltpu.VMEM((heads, toks, dh), bf16),
            pltpu.VMEM((heads, toks, dh + LANES), f32),
            pltpu.VMEM((heads, toks, LANES), f32),
            pltpu.VMEM((spans, own, 1, CAP * BLK), f32),
            pltpu.VMEM((2, BLK * heads, dh), f32),
            pltpu.VMEM((toks, heads, dh), bf16),
            dma((2,)), dma, dma,
            dma((rims,)), dma((rims,)), dma((rims,)), dma((rims,)),
            dma((spans,)), dma((spans,)), dma((spans,)), dma((spans,)),
            dma((own,)),
        ],
        compiler_params=pltpu.CompilerParams(
            collective_id=0, has_side_effects=True, vmem_limit_bytes=62 << 20),
    )(far_list.T, far_count.reshape(1, -1), queries.reshape(toks, heads, dh), keys_values.reshape(-1, own, BLK, heads, dh))
    return result.reshape(queries.shape)


def solution(mesh):
    in_specs = (
        P(("groups", "ctx"), "head", "rep", None),
        P("rep", ("groups", "ctx"), "head", None),
        P("groups", None),
        P("groups"),
    )
    out_specs = P(("groups", "ctx"), "head", "rep", None)
    return jax.shard_map(
        functools.partial(local, mesh.shape["ctx"]),
        mesh=mesh, in_specs=in_specs, out_specs=out_specs, check_vma=False)
```
